32 devices in a mesh: doc: 2 (over core), coarse: 2 (over x), fine: 8 (over z, y).
Axes of the slice: x: 2, y: 2, z: 4, core: 2. Of those that a mesh axis runs over, the one named last changes fastest.
Arguments:
- q_light: bfloat16 [2, 2048, 1024], P('doc', ('coarse', 'fine')), may hold values from -8 to 8
- k_light: bfloat16 [2, 2048, 1024], P('doc', ('coarse', 'fine')), may hold values from -8 to 8
- v_light: bfloat16 [2, 2048, 1024], P('doc', ('coarse', 'fine')), may hold values from -6 to 6
- q_heavy: bfloat16 [2, 2048, 1024], P('doc', ('coarse', 'fine')), may hold values from -8 to 8
- k_heavy: bfloat16 [2, 2048, 1024], P('doc', ('coarse', 'fine')), may hold values from -8 to 8
- v_heavy: bfloat16 [2, 2048, 1024], P('doc', ('coarse', 'fine')), may hold values from -6 to 6
- enc_kv: bfloat16 [2, 2048, 128], P('doc', ('coarse', 'fine')), may hold values from -8 to 8
- dec_queries: bfloat16 [2, 512, 1024], P('doc'), may hold values from -8 to 8
- query_ids: int32 [2, 16], P('doc'), may hold values from 0 to 15, as said below
- key_ids: int32 [2, 16], P('doc'), may hold values from 0 to 15, as said below
Outputs:
- encoded: bfloat16 [2, 2048, 1024], P('doc', ('coarse', 'fine'))
- decoded: bfloat16 [2, 512, 1024], P('doc')
The draws below stay inside these ranges and needn't reach their ends.
Inputs may be any that keep to these rules, and one draw needn't show every extreme that they name: `query_ids`: for each document and each c below the number of coarse groups, entries c * 8 to (c + 1) * 8 - 1 are distinct block numbers among blocks c * 8 to (c + 1) * 8 - 1 (so every block of the group is listed), and entry c * 8 + f is the block assigned to the f-th device of that group. `key_ids`: for each document and each c below the number of coarse groups, entries c * 8 to (c + 1) * 8 - 1 are distinct block numbers among blocks c * 8 * 1 to (c + 1) * 8 - 1.
All inputs are finite; a program needn't handle non-finite values.
Results may differ from the reference program's by a relative error of at most 0.009.
Values may be sent and summed in bfloat16 or wider, within the bound.
A program may use at most 384 MiB of HBM per device.

```python
import jax
import jax.numpy as jnp
from jax import lax

HEADS = 16
HEAD = 64
ROUTED_BLOCK = 128
KGRP = 8
DEC = 512
TOK_DEV = 128
DOCS = 2
DOCUMENT_TOKENS = 2048
N_COARSE = 2
N_FINE = 8


def choose_blocks(key, count):
    per_group = N_FINE * (TOK_DEV // ROUTED_BLOCK)
    blk_dev = TOK_DEV // ROUTED_BLOCK

    def one_group(sub):
        leading_entry, second, third = jax.random.split(sub, 3)
        fullest = jax.random.randint(leading_entry, (), 0, N_FINE)
        scores = jax.random.permutation(second, per_group).astype(jnp.int32)
        local = jnp.arange(per_group, dtype=jnp.int32)
        forced = (local // blk_dev == fullest) & (local % blk_dev < min(blk_dev, count))
        scores = jnp.where(forced, scores + per_group, scores)
        order = jnp.argsort(-scores, stable=True)
        chosen = order[:count].astype(jnp.int32)
        return jax.random.permutation(third, chosen)
    keys = jax.random.split(key, DOCS * N_COARSE)
    picks = jax.vmap(one_group)(keys).reshape(DOCS, N_COARSE, count)
    block_offsets = jnp.arange(N_COARSE, dtype=jnp.int32) * per_group
    return (picks + block_offsets[None, :, None]).reshape(DOCS, N_COARSE * count).astype(jnp.int32)


def draw_query_ids(key, part):
    return choose_blocks(jax.random.fold_in(key, 11), N_FINE)


def draw_key_ids(key, part):
    return choose_blocks(jax.random.fold_in(key, 23), KGRP)


def drawn(key, shape):
    return jnp.clip(jax.random.normal(key, shape, jnp.float32), -6.0, 6.0)


def draw_q_light(key, part):
    field_key = jax.random.fold_in(key, 31)
    shape = (DOCS, DOCUMENT_TOKENS, HEADS * HEAD)
    return drawn(field_key, shape).astype(jnp.bfloat16)


def draw_k_light(key, part):
    field_key = jax.random.fold_in(key, 37)
    shape = (DOCS, DOCUMENT_TOKENS, HEADS * HEAD)
    return drawn(field_key, shape).astype(jnp.bfloat16)


def draw_q_heavy(key, part):
    field_key = jax.random.fold_in(key, 41)
    shape = (DOCS, DOCUMENT_TOKENS, HEADS * HEAD)
    return drawn(field_key, shape).astype(jnp.bfloat16)


def draw_k_heavy(key, part):
    field_key = jax.random.fold_in(key, 43)
    shape = (DOCS, DOCUMENT_TOKENS, HEADS * HEAD)
    return jnp.clip(3.0 * jax.random.normal(field_key, shape, jnp.float32), -8.0, 8.0).astype(jnp.bfloat16)


def draw_enc_kv(key, part):
    field_key = jax.random.fold_in(key, 47)
    shape = (DOCS, DOCUMENT_TOKENS, 2 * HEAD)
    return drawn(field_key, shape).astype(jnp.bfloat16)


def draw_dec_queries(key, part):
    field_key = jax.random.fold_in(key, 53)
    shape = (DOCS, DEC, HEADS * HEAD)
    return drawn(field_key, shape).astype(jnp.bfloat16)


def steps_of(own_key, shape, shards, low, largest):
    level, own = 1.0, jax.random.fold_in(own_key, 6)
    for axis_at, shards_of in shards:
        draws = jnp.exp(jax.random.uniform(jax.random.fold_in(own, axis_at), (shards_of,), jnp.float32, low / len(shards), largest / len(shards)))
        level = level * jnp.repeat(draws, shape[axis_at] // shards_of).reshape([-1 if axis == axis_at else 1 for axis in range(len(shape))])
    return level


def bell_draw(key, shape, deviation, most, shards=(), kind=jnp.bfloat16):
    entries = jax.random.normal(key, shape, jnp.float32) * deviation
    if len(shards) > 0:
        entries = steps_of(key, shape, shards, -0.22, 0.18) * entries
    return jnp.clip(entries, min=-most, max=most).astype(kind)


def setup_inputs(seed: int = 0) -> dict:
    splits = jax.random.split(jax.random.key(seed), 11)
    return {
        "q_light": draw_q_light(jax.random.fold_in(splits[10], 71), 0),
        "k_light": draw_k_light(jax.random.fold_in(splits[10], 71), 0),
        "v_light": bell_draw(splits[2], (DOCS, DOCUMENT_TOKENS, HEADS * HEAD), 1.0, 6.0, ((0, 2), (1, 16))),
        "q_heavy": draw_q_heavy(jax.random.fold_in(splits[10], 71), 0),
        "k_heavy": draw_k_heavy(jax.random.fold_in(splits[10], 71), 0),
        "v_heavy": bell_draw(splits[5], (DOCS, DOCUMENT_TOKENS, HEADS * HEAD), 1.0, 6.0, ((0, 2), (1, 16))),
        "enc_kv": draw_enc_kv(jax.random.fold_in(splits[10], 71), 0),
        "dec_queries": draw_dec_queries(jax.random.fold_in(splits[10], 71), 0),
        "query_ids": draw_query_ids(jax.random.fold_in(splits[10], 71), 0),
        "key_ids": draw_key_ids(jax.random.fold_in(splits[10], 71), 0),
    }


def attend(query, keys, value_rows, mask):
    rows = query.shape[0]
    count = keys.shape[0]
    heads = query.shape[1] // HEAD
    qh = query.reshape(rows, heads, HEAD).transpose(1, 0, 2)
    kh = keys.reshape(count, heads, HEAD).transpose(1, 0, 2)
    vh = value_rows.reshape(count, heads, HEAD).transpose(1, 0, 2)

    def one_head(triple):
        qa, ka, va = triple
        scores = jnp.dot(qa, ka.T, preferred_element_type=jnp.float32) * (HEAD ** -0.5)
        if mask is not None:
            scores = jnp.where(mask, scores, jnp.float32(-1e30))
        peak = jnp.max(scores, axis=1, keepdims=True)
        weights = jnp.exp(scores - peak)
        weights = (weights / jnp.sum(weights, axis=1, keepdims=True)).astype(jnp.bfloat16)
        return jnp.dot(weights, va, preferred_element_type=jnp.float32)

    out = lax.map(one_head, (qh, kh, vh))
    return out.transpose(1, 0, 2).reshape(rows, heads * HEAD)


def light_part(query, keys, value_rows):
    length = query.shape[0]
    width = query.shape[1]
    kpad = jnp.pad(keys, ((ROUTED_BLOCK, ROUTED_BLOCK), (0, 0)))
    padded_values = jnp.pad(value_rows, ((ROUTED_BLOCK, ROUTED_BLOCK), (0, 0)))

    def one_block(index):
        leading_entry = index * ROUTED_BLOCK
        qb = lax.dynamic_slice_in_dim(query, leading_entry, ROUTED_BLOCK)
        kb = lax.dynamic_slice_in_dim(kpad, leading_entry, 3 * ROUTED_BLOCK)
        value_block = lax.dynamic_slice_in_dim(padded_values, leading_entry, 3 * ROUTED_BLOCK)
        qpos = leading_entry + jnp.arange(ROUTED_BLOCK, dtype=jnp.int32)
        kpos = leading_entry - ROUTED_BLOCK + jnp.arange(3 * ROUTED_BLOCK, dtype=jnp.int32)
        mask = (jnp.abs(qpos[:, None] - kpos[None, :]) <= ROUTED_BLOCK - 1) & (kpos[None, :] >= 0) & (kpos[None, :] < length)
        return attend(qb, kb, value_block, mask)

    out = lax.map(one_block, jnp.arange(length // ROUTED_BLOCK, dtype=jnp.int32))
    return out.reshape(length, width)


def heavy_part(query, keys, value_rows, qids, kids):
    length, width = query.shape
    nblk = length // ROUTED_BLOCK
    qblocks = jnp.take(query.reshape(nblk, ROUTED_BLOCK, width), qids.astype(jnp.int32), axis=0)
    kall = jnp.take(keys.reshape(nblk, ROUTED_BLOCK, width), kids.astype(jnp.int32), axis=0).reshape(-1, width)
    vall = jnp.take(value_rows.reshape(nblk, ROUTED_BLOCK, width), kids.astype(jnp.int32), axis=0).reshape(-1, width)
    res = lax.map(lambda qb: attend(qb, kall, vall, None).astype(jnp.bfloat16), qblocks)
    full = jnp.zeros((nblk, ROUTED_BLOCK, width), jnp.bfloat16).at[qids.astype(jnp.int32)].set(res)
    return full.reshape(length, width)


def decoder_part(queries, enc):
    count = queries.shape[0]
    heads = queries.shape[1] // HEAD
    kenc = enc[:, :HEAD]
    venc = enc[:, HEAD:]
    qh = queries.reshape(count, heads, HEAD).transpose(1, 0, 2)

    def one_head(qa):
        scores = jnp.dot(qa, kenc.T, preferred_element_type=jnp.float32) * (HEAD ** -0.5)
        peak = jnp.max(scores, axis=1, keepdims=True)
        weights = jnp.exp(scores - peak)
        total = jnp.sum(weights, axis=1, keepdims=True)
        return jnp.dot(weights.astype(jnp.bfloat16), venc, preferred_element_type=jnp.float32) / total

    out = lax.map(one_head, qh)
    return out.transpose(1, 0, 2).reshape(count, heads * HEAD).astype(jnp.bfloat16)


def reference(q_light, k_light, v_light, q_heavy, k_heavy, v_heavy, enc_kv, dec_queries, query_ids, key_ids):
    encoded = []
    decoded = []
    for doc in range(DOCS):
        light = light_part(q_light[doc], k_light[doc], v_light[doc])
        heavy = heavy_part(q_heavy[doc], k_heavy[doc], v_heavy[doc], query_ids[doc], key_ids[doc])
        encoded.append((light + heavy.astype(jnp.float32)).astype(jnp.bfloat16))
        decoded.append(decoder_part(dec_queries[doc], enc_kv[doc]))
    return jnp.stack(encoded), jnp.stack(decoded)
```

```python
import functools

import jax
import jax.numpy as jnp
from jax import lax
from jax.experimental import pallas as pl
from jax.experimental.pallas import tpu as pltpu
from jax.sharding import PartitionSpec as P

HEAD = 64
PAIR = 2 * HEAD
ROUTED_BLOCK = 128
KGRP = 8
LOW = 2
MESH = pl.DeviceIdType.MESH
NEG = -1e30


def dot_t(a, b):
    return lax.dot_general(a, b, (((1,), (1,)), ((), ())), preferred_element_type=jnp.float32)


def dot(a, b):
    return jnp.dot(a, b, preferred_element_type=jnp.float32)


def stacked_pair(q, low_half):
    q = q * jnp.asarray(HEAD ** (-0.5), q.dtype)
    zero = jnp.zeros_like(q)
    return jnp.concatenate([jnp.where(low_half, q, zero), jnp.where(low_half, zero, q)], axis=0)


def kernel(dims, has_bias, *refs):
    n_coarse, n_fine, tokens, width, dec_rows = dims
    n_seq = n_coarse * n_fine
    n_q = n_fine // LOW
    n_kv = n_coarse * LOW
    heads = width // HEAD
    pairs = heads // 2
    refs = list(refs)
    ql, kl, vl, qh, kh, vh, enc, decq = refs[:8]
    bias_ref = refs[8] if has_bias else None
    (out, dec, encbuf, dq, do, qbuf, kbuf, vbuf, khalo, vhalo, osend, orecv, ssend, srecv,
     wts, light, band, enc_s, enc_r, dec_s, dec_r, q_s, q_r, k_s, k_r, v_s, v_r,
     o_s, o_r, st_s, st_r, h_s, h_r) = refs[8 + has_bias:]

    c = lax.axis_index("coarse")
    f = lax.axis_index("fine")
    here = c * n_fine + f
    me_q = lax.div(f, LOW)
    lo = lax.rem(f, LOW)
    me_kv = c * LOW + lo

    def at_seq(s):
        return {"coarse": lax.div(s, n_fine), "fine": lax.rem(s, n_fine)}

    def at_q(a):
        return {"coarse": c, "fine": a * LOW + lo}

    def at_kv(b):
        return {"coarse": lax.div(b, LOW), "fine": me_q * LOW + lax.rem(b, LOW)}

    def remote(src, dst, ssem, rsem, device):
        return pltpu.make_async_remote_copy(
            src_ref=src, dst_ref=dst, send_sem=ssem, recv_sem=rsem,
            device_id=device, device_id_type=MESH,
        )

    def up(me, d, n):
        return lax.rem(me + d, n)

    def down(me, d, n):
        return lax.rem(me + n - d, n)

    barrier = pltpu.get_barrier_semaphore()

    def greet(d, carry):
        pl.semaphore_signal(barrier, inc=1, device_id=at_seq(up(here, d, n_seq)), device_id_type=MESH)
        return carry

    lax.fori_loop(1, n_seq, greet, 0)
    pl.semaphore_wait(barrier, n_seq - 1)

    def enc_copy(d):
        peer = up(here, d, n_seq)
        return remote(enc, encbuf.at[here], enc_s.at[d], enc_r.at[here], at_seq(peer))

    def enc_arrival(d):
        src = down(here, d, n_seq)
        return remote(enc, encbuf.at[src], enc_s.at[d], enc_r.at[src], at_seq(src))

    def q_copy(d):
        return remote(qh, qbuf.at[me_q], q_s.at[d], q_r.at[me_q], at_q(up(me_q, d, n_q)))

    def q_arrival(d):
        src = up(me_q, d, n_q)
        return remote(qh, qbuf.at[src], q_s.at[d], q_r.at[src], at_q(src))

    def kv_copy(ref, buf, ss, rs, d):
        return remote(ref, buf.at[me_kv], ss.at[d], rs.at[me_kv], at_kv(up(me_kv, d, n_kv)))

    def kv_arrival(ref, buf, ss, rs, d):
        src = down(me_kv, d, n_kv)
        return remote(ref, buf.at[src], ss.at[d], rs.at[src], at_kv(src))

    def o_copy(d):
        peer = up(me_q, d, n_q)
        return (
            remote(osend.at[peer], orecv.at[me_q], o_s.at[d], o_r.at[me_q], at_q(peer)),
            remote(ssend.at[peer], srecv.at[me_q], st_s.at[d], st_r.at[me_q], at_q(peer)),
        )

    def o_arrival(d):
        src = down(me_q, d, n_q)
        return (
            remote(osend.at[src], orecv.at[src], o_s.at[d], o_r.at[src], at_q(src)),
            remote(ssend.at[src], srecv.at[src], st_s.at[d], st_r.at[src], at_q(src)),
        )

    def dec_copy(d):
        peer = up(here, d, n_seq)
        return remote(dec.at[here], dec.at[here], dec_s.at[d], dec_r.at[here], at_seq(peer))

    def dec_arrival(d):
        src = down(here, d, n_seq)
        return remote(dec.at[src], dec.at[src], dec_s.at[d], dec_r.at[src], at_seq(src))

    def halo_copy(side):
        peer = jnp.clip(here + 1 - 2 * side, 0, n_seq - 1)
        return (
            remote(kl, khalo.at[side], h_s.at[side, 0], h_r.at[side, 0], at_seq(peer)),
            remote(vl, vhalo.at[side], h_s.at[side, 1], h_r.at[side, 1], at_seq(peer)),
        )

    def loop(start, stop, body):
        def step(d, carry):
            body(d)
            return carry
        lax.fori_loop(start, stop, step, 0)

    loop(1, n_seq, lambda d: enc_copy(d).start())
    for d in range(1, n_q):
        q_copy(d).start()
    for d in range(1, n_kv):
        kv_copy(kh, kbuf, k_s, k_r, d).start()
        kv_copy(vh, vbuf, v_s, v_r, d).start()
    has_next = here < n_seq - 1
    has_prev = here > 0

    @pl.when(has_next)
    def _():
        for copy in halo_copy(0):
            copy.start()

    @pl.when(has_prev)
    def _():
        for copy in halo_copy(1):
            copy.start()

    encbuf[here] = enc[...]
    qbuf[me_q] = qh[...]
    kbuf[me_kv] = kh[...]
    vbuf[me_kv] = vh[...]
    row = lax.broadcasted_iota(jnp.int32, (tokens, 3 * tokens), 0)
    col = lax.broadcasted_iota(jnp.int32, (tokens, 3 * tokens), 1)
    pos = here * tokens + col - tokens
    seen = (jnp.abs(col - tokens - row) <= ROUTED_BLOCK - 1) & (pos >= 0) & (pos < n_seq * tokens)
    band[...] = jnp.where(seen, jnp.float32(0), jnp.float32(NEG))

    lane_d = lax.broadcasted_iota(jnp.int32, (dec_rows, PAIR), 1)
    for j in range(pairs):
        q = decq[0, :, j * PAIR:(j + 1) * PAIR].astype(jnp.float32) * (HEAD ** (-0.5))
        swapped = pltpu.roll(q, HEAD, 1)
        both = jnp.concatenate(
            [jnp.where(lane_d < HEAD, q, 0.0), jnp.where(lane_d < HEAD, swapped, 0.0)], axis=0
        )
        dq[2 * j * dec_rows:(2 * j + 2) * dec_rows, :] = both.astype(jnp.bfloat16)
    loop(1, n_seq, lambda d: enc_arrival(d).wait_recv())
    d_total = heads * dec_rows
    d_chunk = min(256, d_total)

    def dec_step(i):
        rows = pl.ds(pl.multiple_of(i * d_chunk, d_chunk), d_chunk)
        kv = encbuf[...].reshape(n_seq * tokens, PAIR)
        s = dot_t(dq[rows, :], kv)
        p = jnp.exp(s - jnp.max(s, axis=1, keepdims=True))
        total = jnp.sum(p, axis=1, keepdims=True)
        do[rows, :] = dot(p.astype(jnp.bfloat16), kv) / total

    loop(0, d_total // d_chunk, dec_step)
    for j in range(pairs):
        even = do[2 * j * dec_rows:(2 * j + 1) * dec_rows, :]
        odd = do[(2 * j + 1) * dec_rows:(2 * j + 2) * dec_rows, :]
        dec[here, :, j * PAIR:(j + 1) * PAIR] = jnp.where(
            lane_d < HEAD, pltpu.roll(even, HEAD, 1), odd
        ).astype(jnp.bfloat16)
    loop(1, n_seq, lambda d: dec_copy(d).start())

    low_half = lax.broadcasted_iota(jnp.int32, (tokens, PAIR), 1) < HEAD
    lane = lax.broadcasted_iota(jnp.int32, (tokens, PAIR), 1)
    for d in range(1, n_kv):
        kv_arrival(kh, kbuf, k_s, k_r, d).wait_recv()
        kv_arrival(vh, vbuf, v_s, v_r, d).wait_recv()
    for d in list(range(1, n_q)) + [0]:
        block = up(me_q, d, n_q)
        if d:
            q_arrival(d).wait_recv()

        def pair_step(j, stat):
            cols = pl.ds(pl.multiple_of(j * PAIR, PAIR), PAIR)
            q = stacked_pair(qbuf[block, :, cols], low_half)
            s = dot_t(q, kbuf[:, :, cols].reshape(n_kv * tokens, PAIR))
            if has_bias:
                s = s + bias_ref[0:1, :]
            peak = jnp.max(s, axis=1, keepdims=True)
            p = jnp.exp(s - peak)
            total = jnp.sum(p, axis=1, keepdims=True)
            o = dot(p.astype(jnp.bfloat16), vbuf[:, :, cols].reshape(n_kv * tokens, PAIR)) / total
            lse = peak + jnp.log(total)
            osend[block, :, cols] = jnp.where(low_half, o[:tokens], o[tokens:]).astype(jnp.bfloat16)
            stat = jnp.where(lane == 2 * j, lse[:tokens], stat)
            return jnp.where(lane == 2 * j + 1, lse[tokens:], stat)

        stat = lax.fori_loop(0, pairs, pair_step, jnp.zeros((tokens, PAIR), jnp.float32))
        ssend[block] = stat.T[:heads]
        if d:
            for copy in o_copy(d):
                copy.start()
        else:
            wts[0] = stat

    @pl.when(has_prev)
    def _():
        for copy in halo_copy(0):
            copy.wait_recv()

    @pl.when(jnp.logical_not(has_prev))
    def _():
        khalo[0] = jnp.zeros_like(kl)
        vhalo[0] = jnp.zeros_like(vl)

    @pl.when(has_next)
    def _():
        for copy in halo_copy(1):
            copy.wait_recv()

    @pl.when(jnp.logical_not(has_next))
    def _():
        khalo[1] = jnp.zeros_like(kl)
        vhalo[1] = jnp.zeros_like(vl)

    def light_step(j):
        cols = pl.ds(pl.multiple_of(j * PAIR, PAIR), PAIR)
        q = stacked_pair(ql[:, cols], low_half)
        keys = jnp.concatenate([khalo[0, :, cols], kl[:, cols], khalo[1, :, cols]], axis=0)
        rows = jnp.concatenate([vhalo[0, :, cols], vl[:, cols], vhalo[1, :, cols]], axis=0)
        mask = band[...]
        s = dot_t(q, keys) + jnp.concatenate([mask, mask], axis=0)
        p = jnp.exp(s - jnp.max(s, axis=1, keepdims=True))
        total = jnp.sum(p, axis=1, keepdims=True)
        o = dot(p.astype(jnp.bfloat16), rows) / total
        light[:, cols] = jnp.where(low_half, o[:tokens], o[tokens:])

    loop(0, pairs, light_step)

    for d in range(1, n_q):
        for copy in o_arrival(d):
            copy.wait_recv()
        pad = jnp.zeros((PAIR - heads, tokens), jnp.float32)
        wts[d] = jnp.concatenate([srecv[down(me_q, d, n_q)], pad], axis=0).T
    top = wts[0]
    for d in range(1, n_q):
        top = jnp.maximum(top, wts[d])
    norm = jnp.zeros_like(top)
    for d in range(n_q):
        share = jnp.exp(wts[d] - top)
        wts[d] = share
        norm = norm + share
    for d in range(n_q):
        wts[d] = wts[d] / norm

    def join_step(j):
        cols = pl.ds(pl.multiple_of(j * PAIR, PAIR), PAIR)
        acc = jnp.zeros((tokens, PAIR), jnp.float32)
        for d in range(n_q):
            part = osend[me_q, :, cols] if d == 0 else orecv[down(me_q, d, n_q), :, cols]
            w = wts[d]
            even = jnp.sum(jnp.where(lane == 2 * j, w, 0.0), axis=1, keepdims=True)
            odd = jnp.sum(jnp.where(lane == 2 * j + 1, w, 0.0), axis=1, keepdims=True)
            acc = acc + jnp.where(low_half, even, odd) * part.astype(jnp.float32)
        heavy = acc.astype(jnp.bfloat16).astype(jnp.float32)
        out[:, cols] = (light[:, cols] + heavy).astype(jnp.bfloat16)

    loop(0, pairs, join_step)

    loop(1, n_seq, lambda d: dec_arrival(d).wait_recv())
    loop(1, n_seq, lambda d: enc_copy(d).wait_send())
    loop(1, n_seq, lambda d: dec_copy(d).wait_send())
    for d in range(1, n_q):
        q_copy(d).wait_send()
        for copy in o_copy(d):
            copy.wait_send()
    for d in range(1, n_kv):
        kv_copy(kh, kbuf, k_s, k_r, d).wait_send()
        kv_copy(vh, vbuf, v_s, v_r, d).wait_send()

    @pl.when(has_next)
    def _():
        for copy in halo_copy(0):
            copy.wait_send()

    @pl.when(has_prev)
    def _():
        for copy in halo_copy(1):
            copy.wait_send()


def local(
    q_light, k_light, v_light, q_heavy, k_heavy, v_heavy, enc_kv, dec_queries, query_ids, key_ids
):
    _, tokens, width = q_light.shape
    n_coarse = lax.axis_size("coarse")
    n_fine = lax.axis_size("fine")
    n_seq = n_coarse * n_fine
    n_q = n_fine // LOW
    n_kv = n_coarse * LOW
    heads = width // HEAD
    count = dec_queries.shape[1]
    dec_rows = count // n_seq
    here = lax.axis_index(("coarse", "fine"))
    mine = lax.dynamic_slice_in_dim(dec_queries.reshape(n_seq, dec_rows, width), here, 1)
    args = [q_light[0], k_light[0], v_light[0], q_heavy[0], k_heavy[0], v_heavy[0], enc_kv[0], mine]
    has_bias = key_ids.shape[1] != n_seq
    if has_bias:
        high = lax.div(lax.axis_index("fine"), LOW)
        member = jnp.arange(n_kv, dtype=jnp.int32)
        blocks = (member // LOW) * n_fine + high * LOW + member % LOW
        listed = jnp.any(blocks[:, None] == key_ids[0][None, :], axis=1)
        bias = jnp.repeat(jnp.where(listed, 0.0, NEG).astype(jnp.float32), tokens)
        args.append(jnp.broadcast_to(bias[None], (8, n_kv * tokens)))
    bf16, f32 = jnp.bfloat16, jnp.float32
    dma = pltpu.SemaphoreType.DMA
    vmem = pl.BlockSpec(memory_space=pltpu.VMEM)
    encoded, decoded = pl.pallas_call(
        functools.partial(kernel, (n_coarse, n_fine, tokens, width, dec_rows), has_bias),
        out_shape=(
            jax.ShapeDtypeStruct((tokens, width), bf16),
            jax.ShapeDtypeStruct((n_seq, dec_rows, width), bf16),
        ),
        in_specs=[vmem] * len(args),
        out_specs=(vmem, vmem),
        scratch_shapes=[
            pltpu.VMEM((n_seq, tokens, PAIR), bf16),
            pltpu.VMEM((heads * dec_rows, PAIR), bf16),
            pltpu.VMEM((heads * dec_rows, PAIR), f32),
            pltpu.VMEM((n_q, tokens, width), bf16),
            pltpu.VMEM((n_kv, tokens, width), bf16),
            pltpu.VMEM((n_kv, tokens, width), bf16),
            pltpu.VMEM((2, tokens, width), bf16),
            pltpu.VMEM((2, tokens, width), bf16),
            pltpu.VMEM((n_q, tokens, width), bf16),
            pltpu.VMEM((n_q, tokens, width), bf16),
            pltpu.VMEM((n_q, heads, tokens), f32),
            pltpu.VMEM((n_q, heads, tokens), f32),
            pltpu.VMEM((n_q, tokens, PAIR), f32),
            pltpu.VMEM((tokens, width), f32),
            pltpu.VMEM((tokens, 3 * tokens), f32),
            dma((n_seq,)), dma((n_seq,)),
            dma((n_seq,)), dma((n_seq,)),
            dma((n_q,)), dma((n_q,)),
            dma((n_kv,)), dma((n_kv,)),
            dma((n_kv,)), dma((n_kv,)),
            dma((n_q,)), dma((n_q,)),
            dma((n_q,)), dma((n_q,)),
            dma((2, 2)), dma((2, 2)),
        ],
        compiler_params=pltpu.CompilerParams(
            collective_id=0, has_side_effects=True, vmem_limit_bytes=60 * 1024 * 1024
        ),
    )(*args)
    return encoded[None], decoded.reshape(1, count, width)


def solution(mesh):
    rows = P("doc", ("coarse", "fine"), None)
    placed = (rows,) * 7 + (P("doc", None, None), P("doc", None), P("doc", None))
    return jax.shard_map(
        local,
        mesh=mesh,
        in_specs=placed,
        out_specs=(rows, P("doc", None, None)),
        check_vma=False,
    )
```

```python
import functools

import jax
import jax.numpy as jnp
from jax import lax
from jax.experimental import pallas as pl
from jax.experimental.pallas import tpu as pltpu
from jax.sharding import PartitionSpec as P

HEAD = 64
PAIR = 2 * HEAD
ROUTED_BLOCK = 128
KGRP = 8
LOW = 2
MESH = pl.DeviceIdType.MESH
NEG = -1e30


def dot_t(a, b):
    return lax.dot_general(a, b, (((1,), (1,)), ((), ())), preferred_element_type=jnp.float32)


def dot(a, b):
    return jnp.dot(a, b, preferred_element_type=jnp.float32)


def stacked_pair(q, low_half):
    q = q * jnp.asarray(HEAD ** (-0.5), q.dtype)
    zero = jnp.zeros_like(q)
    return jnp.concatenate([jnp.where(low_half, q, zero), jnp.where(low_half, zero, q)], axis=0)


def kernel(dims, has_bias, *refs):
    n_coarse, n_fine, tokens, width, dec_rows = dims
    n_seq = n_coarse * n_fine
    n_q = n_fine // LOW
    n_kv = n_coarse * LOW
    heads = width // HEAD
    pairs = heads // 2
    refs = list(refs)
    ql, kl, vl, qh, kh, vh, enc, decq = refs[:8]
    bias_ref = refs[8] if has_bias else None
    (out, dec, encbuf, dq, do, qbuf, kbuf, vbuf, khalo, vhalo, osend, orecv, ssend, srecv,
     wts, light, band, enc_s, enc_r, dec_s, dec_r, q_s, q_r, o_s, o_r, st_s, st_r, h_s, h_r,
     ek_s, ek_r, dk_s, dk_r, k_s, k_r, v_s, v_r) = refs[8 + has_bias:]

    c = lax.axis_index("coarse")
    f = lax.axis_index("fine")
    here = c * n_fine + f
    me_q = lax.div(f, LOW)
    lo = lax.rem(f, LOW)
    me_kv = c * LOW + lo

    def at_seq(s):
        return {"coarse": lax.div(s, n_fine), "fine": lax.rem(s, n_fine)}

    def at_q(a):
        return {"coarse": c, "fine": a * LOW + lo}

    def at_kv(b):
        return {"coarse": lax.div(b, LOW), "fine": me_q * LOW + lax.rem(b, LOW)}

    def remote(src, dst, ssem, rsem, device):
        return pltpu.make_async_remote_copy(
            src_ref=src, dst_ref=dst, send_sem=ssem, recv_sem=rsem,
            device_id=device, device_id_type=MESH,
        )

    def up(me, d, n):
        return lax.rem(me + d, n)

    def down(me, d, n):
        return lax.rem(me + n - d, n)

    barrier = pltpu.get_barrier_semaphore()

    def greet(d, carry):
        pl.semaphore_signal(barrier, inc=1, device_id=at_seq(up(here, d, n_seq)), device_id_type=MESH)
        return carry

    lax.fori_loop(1, n_seq, greet, 0)
    pl.semaphore_wait(barrier, n_seq - 1)

    def enc_copy(d):
        mine = encbuf.at[me_kv, me_q]
        return remote(enc, mine, enc_s.at[d], enc_r.at[me_q], at_q(up(me_q, d, n_q)))

    def enc_arrival(d):
        src = down(me_q, d, n_q)
        return remote(enc, encbuf.at[me_kv, src], enc_s.at[d], enc_r.at[src], at_q(src))

    def dec_copy(d):
        mine = dec.at[me_kv, me_q]
        return remote(mine, mine, dec_s.at[d], dec_r.at[me_q], at_q(up(me_q, d, n_q)))

    def dec_arrival(d):
        src = down(me_q, d, n_q)
        part = dec.at[me_kv, src]
        return remote(part, part, dec_s.at[d], dec_r.at[src], at_q(src))

    def q_copy(block, way):
        peer = jnp.clip(me_q + way, 0, n_q - 1)
        return remote(qbuf.at[block], qbuf.at[block], q_s.at[block], q_r.at[block], at_q(peer))

    def own_q(way):
        peer = jnp.clip(me_q + way, 0, n_q - 1)
        return remote(qh, qbuf.at[me_q], q_s.at[n_q + int(way > 0)], q_r.at[me_q], at_q(peer))

    def q_step(t):
        for way in (1, -1):
            src = me_q - way * t
            block = jnp.clip(src, 0, n_q - 1)

            @pl.when((src >= 0) & (src < n_q))
            def _():
                q_copy(block, -way).wait_recv()

                @pl.when((me_q + way >= 0) & (me_q + way < n_q))
                def _():
                    q_copy(block, way).start()

    other = c * LOW + 1 - lo

    def plane(src, buf, ss, rs):
        def low():
            return remote(src, buf.at[me_kv], ss.at[0, 0], rs.at[me_kv], at_kv(other))

        def far(d, relay):
            block = other if relay else me_kv
            peer = up(c, d, n_coarse) * LOW + lo
            return remote(buf.at[other] if relay else src, buf.at[block],
                          ss.at[int(relay), d], rs.at[block], at_kv(peer))

        def arrival(block):
            return remote(src, buf.at[block], ss.at[0, 0], rs.at[block], at_kv(block))

        def begin():
            low().start()
            for d in range(1, n_coarse):
                far(d, False).start()

        def relay():
            arrival(other).wait_recv()
            for d in range(1, n_coarse):
                far(d, True).start()

        def arrive():
            for d in range(1, n_coarse):
                column = up(c, d, n_coarse) * LOW
                for part in range(LOW):
                    arrival(column + part).wait_recv()

        def sent():
            low().wait_send()
            for d in range(1, n_coarse):
                far(d, False).wait_send()
                far(d, True).wait_send()

        return begin, relay, arrive, sent

    enc_plane = plane(encbuf.at[me_kv], encbuf, ek_s, ek_r)
    dec_plane = plane(dec.at[me_kv], dec, dk_s, dk_r)
    k_plane = plane(kh, kbuf, k_s, k_r)
    v_plane = plane(vh, vbuf, v_s, v_r)

    def o_copy(d):
        peer = up(me_q, d, n_q)
        return (
            remote(osend.at[peer], orecv.at[me_q], o_s.at[d], o_r.at[me_q], at_q(peer)),
            remote(ssend.at[peer], srecv.at[me_q], st_s.at[d], st_r.at[me_q], at_q(peer)),
        )

    def o_arrival(d):
        src = down(me_q, d, n_q)
        return (
            remote(osend.at[src], orecv.at[src], o_s.at[d], o_r.at[src], at_q(src)),
            remote(ssend.at[src], srecv.at[src], st_s.at[d], st_r.at[src], at_q(src)),
        )

    def halo_copy(side):
        peer = jnp.clip(here + 1 - 2 * side, 0, n_seq - 1)
        return (
            remote(kl, khalo.at[side], h_s.at[side, 0], h_r.at[side, 0], at_seq(peer)),
            remote(vl, vhalo.at[side], h_s.at[side, 1], h_r.at[side, 1], at_seq(peer)),
        )

    def loop(start, stop, body):
        def step(d, carry):
            body(d)
            return carry
        lax.fori_loop(start, stop, step, 0)

    for d in range(1, n_q):
        enc_copy(d).start()
    k_plane[0]()
    v_plane[0]()
    has_up = me_q < n_q - 1
    has_down = me_q > 0

    @pl.when(has_up)
    def _():
        own_q(1).start()

    @pl.when(has_down)
    def _():
        own_q(-1).start()

    has_next = here < n_seq - 1
    has_prev = here > 0

    encbuf[me_kv, me_q] = enc[...]
    qbuf[me_q] = qh[...]
    kbuf[me_kv] = kh[...]
    vbuf[me_kv] = vh[...]
    row = lax.broadcasted_iota(jnp.int32, (tokens, 3 * tokens), 0)
    col = lax.broadcasted_iota(jnp.int32, (tokens, 3 * tokens), 1)
    pos = here * tokens + col - tokens
    seen = (jnp.abs(col - tokens - row) <= ROUTED_BLOCK - 1) & (pos >= 0) & (pos < n_seq * tokens)
    band[...] = jnp.where(seen, jnp.float32(0), jnp.float32(NEG))

    lane_d = lax.broadcasted_iota(jnp.int32, (dec_rows, PAIR), 1)
    for j in range(pairs):
        q = decq[0, :, j * PAIR:(j + 1) * PAIR].astype(jnp.float32) * (HEAD ** (-0.5))
        swapped = pltpu.roll(q, HEAD, 1)
        both = jnp.concatenate(
            [jnp.where(lane_d < HEAD, q, 0.0), jnp.where(lane_d < HEAD, swapped, 0.0)], axis=0
        )
        dq[2 * j * dec_rows:(2 * j + 2) * dec_rows, :] = both.astype(jnp.bfloat16)
    for d in range(1, n_q):
        enc_arrival(d).wait_recv()
    enc_plane[0]()
    q_step(1)
    enc_plane[1]()
    k_plane[1]()
    v_plane[1]()

    @pl.when(has_next)
    def _():
        for copy in halo_copy(0):
            copy.start()

    @pl.when(has_prev)
    def _():
        for copy in halo_copy(1):
            copy.start()

    for t in range(2, n_q - 1):
        q_step(t)
    enc_plane[2]()
    d_total = heads * dec_rows
    d_chunk = min(256, d_total)

    def dec_step(i):
        rows = pl.ds(pl.multiple_of(i * d_chunk, d_chunk), d_chunk)
        kv = encbuf[...].reshape(n_seq * tokens, PAIR)
        s = dot_t(dq[rows, :], kv)
        p = jnp.exp(s - jnp.max(s, axis=1, keepdims=True))
        total = jnp.sum(p, axis=1, keepdims=True)
        do[rows, :] = dot(p.astype(jnp.bfloat16), kv) / total

    loop(0, d_total // d_chunk, dec_step)
    for j in range(pairs):
        even = do[2 * j * dec_rows:(2 * j + 1) * dec_rows, :]
        odd = do[(2 * j + 1) * dec_rows:(2 * j + 2) * dec_rows, :]
        dec[me_kv, me_q, :, j * PAIR:(j + 1) * PAIR] = jnp.where(
            lane_d < HEAD, pltpu.roll(even, HEAD, 1), odd
        ).astype(jnp.bfloat16)
    for d in range(1, n_q):
        dec_copy(d).start()

    low_half = lax.broadcasted_iota(jnp.int32, (tokens, PAIR), 1) < HEAD
    lane = lax.broadcasted_iota(jnp.int32, (tokens, PAIR), 1)
    if n_q > 2:
        q_step(n_q - 1)
    for d in range(1, n_q):
        dec_arrival(d).wait_recv()
    dec_plane[0]()
    k_plane[2]()
    v_plane[2]()
    for d in list(range(1, n_q)) + [0]:
        block = up(me_q, d, n_q)
        if d == 0:
            dec_plane[1]()

        def pair_step(j, stat):
            cols = pl.ds(pl.multiple_of(j * PAIR, PAIR), PAIR)
            q = stacked_pair(qbuf[block, :, cols], low_half)
            s = dot_t(q, kbuf[:, :, cols].reshape(n_kv * tokens, PAIR))
            if has_bias:
                s = s + bias_ref[0:1, :]
            peak = jnp.max(s, axis=1, keepdims=True)
            p = jnp.exp(s - peak)
            total = jnp.sum(p, axis=1, keepdims=True)
            o = dot(p.astype(jnp.bfloat16), vbuf[:, :, cols].reshape(n_kv * tokens, PAIR)) / total
            lse = peak + jnp.log(total)
            osend[block, :, cols] = jnp.where(low_half, o[:tokens], o[tokens:]).astype(jnp.bfloat16)
            stat = jnp.where(lane == 2 * j, lse[:tokens], stat)
            return jnp.where(lane == 2 * j + 1, lse[tokens:], stat)

        stat = lax.fori_loop(0, pairs, pair_step, jnp.zeros((tokens, PAIR), jnp.float32))
        ssend[block] = stat.T[:heads]
        if d:
            for copy in o_copy(d):
                copy.start()
        else:
            wts[0] = stat

    @pl.when(has_prev)
    def _():
        for copy in halo_copy(0):
            copy.wait_recv()

    @pl.when(jnp.logical_not(has_prev))
    def _():
        khalo[0] = jnp.zeros_like(kl)
        vhalo[0] = jnp.zeros_like(vl)

    @pl.when(has_next)
    def _():
        for copy in halo_copy(1):
            copy.wait_recv()

    @pl.when(jnp.logical_not(has_next))
    def _():
        khalo[1] = jnp.zeros_like(kl)
        vhalo[1] = jnp.zeros_like(vl)

    def light_step(j):
        cols = pl.ds(pl.multiple_of(j * PAIR, PAIR), PAIR)
        q = stacked_pair(ql[:, cols], low_half)
        keys = jnp.concatenate([khalo[0, :, cols], kl[:, cols], khalo[1, :, cols]], axis=0)
        rows = jnp.concatenate([vhalo[0, :, cols], vl[:, cols], vhalo[1, :, cols]], axis=0)
        mask = band[...]
        s = dot_t(q, keys) + jnp.concatenate([mask, mask], axis=0)
        p = jnp.exp(s - jnp.max(s, axis=1, keepdims=True))
        total = jnp.sum(p, axis=1, keepdims=True)
        o = dot(p.astype(jnp.bfloat16), rows) / total
        light[:, cols] = jnp.where(low_half, o[:tokens], o[tokens:])

    loop(0, pairs, light_step)

    for d in range(1, n_q):
        for copy in o_arrival(d):
            copy.wait_recv()
        pad = jnp.zeros((PAIR - heads, tokens), jnp.float32)
        wts[d] = jnp.concatenate([srecv[down(me_q, d, n_q)], pad], axis=0).T
    top = wts[0]
    for d in range(1, n_q):
        top = jnp.maximum(top, wts[d])
    norm = jnp.zeros_like(top)
    for d in range(n_q):
        share = jnp.exp(wts[d] - top)
        wts[d] = share
        norm = norm + share
    for d in range(n_q):
        wts[d] = wts[d] / norm

    def join_step(j):
        cols = pl.ds(pl.multiple_of(j * PAIR, PAIR), PAIR)
        acc = jnp.zeros((tokens, PAIR), jnp.float32)
        for d in range(n_q):
            part = osend[me_q, :, cols] if d == 0 else orecv[down(me_q, d, n_q), :, cols]
            w = wts[d]
            even = jnp.sum(jnp.where(lane == 2 * j, w, 0.0), axis=1, keepdims=True)
            odd = jnp.sum(jnp.where(lane == 2 * j + 1, w, 0.0), axis=1, keepdims=True)
            acc = acc + jnp.where(low_half, even, odd) * part.astype(jnp.float32)
        heavy = acc.astype(jnp.bfloat16).astype(jnp.float32)
        out[:, cols] = (light[:, cols] + heavy).astype(jnp.bfloat16)

    loop(0, pairs, join_step)

    dec_plane[2]()
    for part in (enc_plane, dec_plane, k_plane, v_plane):
        part[3]()
    for d in range(1, n_q):
        enc_copy(d).wait_send()
        dec_copy(d).wait_send()
        for copy in o_copy(d):
            copy.wait_send()

    @pl.when(has_up)
    def _():
        own_q(1).wait_send()

    @pl.when(has_down)
    def _():
        own_q(-1).wait_send()

    for t in range(1, n_q - 1):
        for way in (1, -1):
            src = me_q - way * t

            @pl.when((src >= 0) & (src < n_q) & (me_q + way >= 0) & (me_q + way < n_q))
            def _():
                q_copy(jnp.clip(src, 0, n_q - 1), way).wait_send()

    @pl.when(has_next)
    def _():
        for copy in halo_copy(0):
            copy.wait_send()

    @pl.when(has_prev)
    def _():
        for copy in halo_copy(1):
            copy.wait_send()


def local(
    q_light, k_light, v_light, q_heavy, k_heavy, v_heavy, enc_kv, dec_queries, query_ids, key_ids
):
    _, tokens, width = q_light.shape
    n_coarse = lax.axis_size("coarse")
    n_fine = lax.axis_size("fine")
    n_seq = n_coarse * n_fine
    n_q = n_fine // LOW
    n_kv = n_coarse * LOW
    heads = width // HEAD
    count = dec_queries.shape[1]
    dec_rows = count // n_seq
    fine = lax.axis_index("fine")
    slot = (lax.axis_index("coarse") * LOW + fine % LOW) * n_q + fine // LOW
    mine = lax.dynamic_slice_in_dim(dec_queries.reshape(n_seq, dec_rows, width), slot, 1)
    args = [q_light[0], k_light[0], v_light[0], q_heavy[0], k_heavy[0], v_heavy[0], enc_kv[0], mine]
    has_bias = key_ids.shape[1] != n_seq
    if has_bias:
        high = lax.div(lax.axis_index("fine"), LOW)
        member = jnp.arange(n_kv, dtype=jnp.int32)
        blocks = (member // LOW) * n_fine + high * LOW + member % LOW
        listed = jnp.any(blocks[:, None] == key_ids[0][None, :], axis=1)
        bias = jnp.repeat(jnp.where(listed, 0.0, NEG).astype(jnp.float32), tokens)
        args.append(jnp.broadcast_to(bias[None], (8, n_kv * tokens)))
    bf16, f32 = jnp.bfloat16, jnp.float32
    dma = pltpu.SemaphoreType.DMA
    vmem = pl.BlockSpec(memory_space=pltpu.VMEM)
    encoded, decoded = pl.pallas_call(
        functools.partial(kernel, (n_coarse, n_fine, tokens, width, dec_rows), has_bias),
        out_shape=(
            jax.ShapeDtypeStruct((tokens, width), bf16),
            jax.ShapeDtypeStruct((n_kv, n_q, dec_rows, width), bf16),
        ),
        in_specs=[vmem] * len(args),
        out_specs=(vmem, vmem),
        scratch_shapes=[
            pltpu.VMEM((n_kv, n_q, tokens, PAIR), bf16),
            pltpu.VMEM((heads * dec_rows, PAIR), bf16),
            pltpu.VMEM((heads * dec_rows, PAIR), f32),
            pltpu.VMEM((n_q, tokens, width), bf16),
            pltpu.VMEM((n_kv, tokens, width), bf16),
            pltpu.VMEM((n_kv, tokens, width), bf16),
            pltpu.VMEM((2, tokens, width), bf16),
            pltpu.VMEM((2, tokens, width), bf16),
            pltpu.VMEM((n_q, tokens, width), bf16),
            pltpu.VMEM((n_q, tokens, width), bf16),
            pltpu.VMEM((n_q, heads, tokens), f32),
            pltpu.VMEM((n_q, heads, tokens), f32),
            pltpu.VMEM((n_q, tokens, PAIR), f32),
            pltpu.VMEM((tokens, width), f32),
            pltpu.VMEM((tokens, 3 * tokens), f32),
            dma((n_q,)), dma((n_q,)),
            dma((n_q,)), dma((n_q,)),
            dma((n_q + 2,)), dma((n_q,)),
            dma((n_q,)), dma((n_q,)),
            dma((n_q,)), dma((n_q,)),
            dma((2, 2)), dma((2, 2)),
            dma((2, n_coarse)), dma((n_kv,)),
            dma((2, n_coarse)), dma((n_kv,)),
            dma((2, n_coarse)), dma((n_kv,)),
            dma((2, n_coarse)), dma((n_kv,)),
        ],
        compiler_params=pltpu.CompilerParams(
            collective_id=0, has_side_effects=True, vmem_limit_bytes=60 * 1024 * 1024
        ),
    )(*args)
    return encoded[None], decoded.reshape(1, count, width)


def solution(mesh):
    rows = P("doc", ("coarse", "fine"), None)
    placed = (rows,) * 7 + (P("doc", None, None), P("doc", None), P("doc", None))
    return jax.shard_map(
        local,
        mesh=mesh,
        in_specs=placed,
        out_specs=(rows, P("doc", None, None)),
        check_vma=False,
    )
```

```python
import functools

import jax
import jax.numpy as jnp
from jax import lax
from jax.experimental import pallas as pl
from jax.experimental.pallas import tpu as pltpu
from jax.sharding import PartitionSpec as P

HEAD = 64
PAIR = 2 * HEAD
ROUTED_BLOCK = 128
KGRP = 8
LOW = 2
MESH = pl.DeviceIdType.MESH
NEG = -1e30


def dot_t(a, b):
    return lax.dot_general(a, b, (((1,), (1,)), ((), ())), preferred_element_type=jnp.float32)


def dot(a, b):
    return jnp.dot(a, b, preferred_element_type=jnp.float32)


def stacked_pair(q, low_half):
    q = q * jnp.asarray(HEAD ** (-0.5), q.dtype)
    zero = jnp.zeros_like(q)
    return jnp.concatenate([jnp.where(low_half, q, zero), jnp.where(low_half, zero, q)], axis=0)


def kernel(dims, has_bias, *refs):
    n_coarse, n_fine, tokens, width, dec_rows = dims
    n_seq = n_coarse * n_fine
    n_q = n_fine // LOW
    n_kv = n_coarse * LOW
    heads = width // HEAD
    pairs = heads // 2
    refs = list(refs)
    ql, kl, vl, qh, kh, vh, enc, decq = refs[:8]
    bias_ref = refs[8] if has_bias else None
    (out, dec, encbuf, dq, do, qbuf, kbuf, vbuf, khalo, vhalo, osend, orecv, ssend, srecv,
     wts, light, band, enc_s, enc_r, dec_s, dec_r, q_s, q_r, o_s, o_r, st_s, st_r, h_s, h_r,
     ek_s, ek_r, dk_s, dk_r, k_s, k_r, v_s, v_r, drows, load_s) = refs[8 + has_bias:]

    c = lax.axis_index("coarse")
    f = lax.axis_index("fine")
    here = c * n_fine + f
    me_q = lax.div(f, LOW)
    lo = lax.rem(f, LOW)
    me_kv = c * LOW + lo

    def at_seq(s):
        return {"coarse": lax.div(s, n_fine), "fine": lax.rem(s, n_fine)}

    def at_q(a):
        return {"coarse": c, "fine": a * LOW + lo}

    def at_kv(b):
        return {"coarse": lax.div(b, LOW), "fine": me_q * LOW + lax.rem(b, LOW)}

    def remote(src, dst, ssem, rsem, device):
        return pltpu.make_async_remote_copy(
            src_ref=src, dst_ref=dst, send_sem=ssem, recv_sem=rsem,
            device_id=device, device_id_type=MESH,
        )

    def up(me, d, n):
        return lax.rem(me + d, n)

    def down(me, d, n):
        return lax.rem(me + n - d, n)

    load = pltpu.make_async_copy(decq.at[me_kv, me_q], drows, load_s)
    load.start()
    barrier = pltpu.get_barrier_semaphore()

    def greet(d, carry):
        pl.semaphore_signal(barrier, inc=1, device_id=at_seq(up(here, d, n_seq)), device_id_type=MESH)
        return carry

    lax.fori_loop(1, n_seq, greet, 0)
    pl.semaphore_wait(barrier, n_seq - 1)

    def enc_copy(d):
        mine = encbuf.at[me_kv, me_q]
        return remote(enc, mine, enc_s.at[d], enc_r.at[me_q], at_q(up(me_q, d, n_q)))

    def enc_arrival(d):
        src = down(me_q, d, n_q)
        return remote(enc, encbuf.at[me_kv, src], enc_s.at[d], enc_r.at[src], at_q(src))

    def dec_copy(d):
        mine = dec.at[me_kv, me_q]
        return remote(mine, mine, dec_s.at[d], dec_r.at[me_q], at_q(up(me_q, d, n_q)))

    def dec_arrival(d):
        src = down(me_q, d, n_q)
        part = dec.at[me_kv, src]
        return remote(part, part, dec_s.at[d], dec_r.at[src], at_q(src))

    def q_copy(block, way):
        peer = jnp.clip(me_q + way, 0, n_q - 1)
        return remote(qbuf.at[block], qbuf.at[block], q_s.at[block], q_r.at[block], at_q(peer))

    def own_q(way):
        peer = jnp.clip(me_q + way, 0, n_q - 1)
        return remote(qh, qbuf.at[me_q], q_s.at[n_q + int(way > 0)], q_r.at[me_q], at_q(peer))

    def q_step(t):
        for way in (1, -1):
            src = me_q - way * t
            block = jnp.clip(src, 0, n_q - 1)

            @pl.when((src >= 0) & (src < n_q))
            def _():
                q_copy(block, -way).wait_recv()

                @pl.when((me_q + way >= 0) & (me_q + way < n_q))
                def _():
                    q_copy(block, way).start()

    other = c * LOW + 1 - lo

    def plane(src, buf, ss, rs):
        def low():
            return remote(src, buf.at[me_kv], ss.at[0, 0], rs.at[me_kv], at_kv(other))

        def far(d, relay):
            block = other if relay else me_kv
            peer = up(c, d, n_coarse) * LOW + lo
            return remote(buf.at[other] if relay else src, buf.at[block],
                          ss.at[int(relay), d], rs.at[block], at_kv(peer))

        def arrival(block):
            return remote(src, buf.at[block], ss.at[0, 0], rs.at[block], at_kv(block))

        def begin():
            low().start()
            for d in range(1, n_coarse):
                far(d, False).start()

        def relay():
            arrival(other).wait_recv()
            for d in range(1, n_coarse):
                far(d, True).start()

        def arrive():
            for d in range(1, n_coarse):
                column = up(c, d, n_coarse) * LOW
                for part in range(LOW):
                    arrival(column + part).wait_recv()

        def sent():
            low().wait_send()
            for d in range(1, n_coarse):
                far(d, False).wait_send()
                far(d, True).wait_send()

        return begin, relay, arrive, sent

    enc_plane = plane(encbuf.at[me_kv], encbuf, ek_s, ek_r)
    dec_plane = plane(dec.at[me_kv], dec, dk_s, dk_r)
    k_plane = plane(kh, kbuf, k_s, k_r)
    v_plane = plane(vh, vbuf, v_s, v_r)

    def o_copy(d):
        peer = up(me_q, d, n_q)
        return (
            remote(osend.at[peer], orecv.at[me_q], o_s.at[d], o_r.at[me_q], at_q(peer)),
            remote(ssend.at[peer], srecv.at[me_q], st_s.at[d], st_r.at[me_q], at_q(peer)),
        )

    def o_arrival(d):
        src = down(me_q, d, n_q)
        return (
            remote(osend.at[src], orecv.at[src], o_s.at[d], o_r.at[src], at_q(src)),
            remote(ssend.at[src], srecv.at[src], st_s.at[d], st_r.at[src], at_q(src)),
        )

    def halo_copy(side):
        peer = jnp.clip(here + 1 - 2 * side, 0, n_seq - 1)
        return (
            remote(kl, khalo.at[side], h_s.at[side, 0], h_r.at[side, 0], at_seq(peer)),
            remote(vl, vhalo.at[side], h_s.at[side, 1], h_r.at[side, 1], at_seq(peer)),
        )

    def loop(start, stop, body):
        def step(d, carry):
            body(d)
            return carry
        lax.fori_loop(start, stop, step, 0)

    for d in range(1, n_q):
        enc_copy(d).start()
    k_plane[0]()
    has_up = me_q < n_q - 1
    has_down = me_q > 0

    @pl.when(has_up)
    def _():
        own_q(1).start()

    @pl.when(has_down)
    def _():
        own_q(-1).start()

    has_next = here < n_seq - 1
    has_prev = here > 0

    encbuf[me_kv, me_q] = enc[...]
    for d in range(1, n_q):
        enc_arrival(d).wait_recv()
    enc_plane[0]()
    v_plane[0]()

    @pl.when(has_next)
    def _():
        for copy in halo_copy(0):
            copy.start()

    @pl.when(has_prev)
    def _():
        for copy in halo_copy(1):
            copy.start()

    qbuf[me_q] = qh[...]
    kbuf[me_kv] = kh[...]
    vbuf[me_kv] = vh[...]
    row = lax.broadcasted_iota(jnp.int32, (tokens, 3 * tokens), 0)
    col = lax.broadcasted_iota(jnp.int32, (tokens, 3 * tokens), 1)
    pos = here * tokens + col - tokens
    seen = (jnp.abs(col - tokens - row) <= ROUTED_BLOCK - 1) & (pos >= 0) & (pos < n_seq * tokens)
    band[...] = jnp.where(seen, jnp.float32(0), jnp.float32(NEG))

    load.wait()
    lane_d = lax.broadcasted_iota(jnp.int32, (dec_rows, PAIR), 1)
    for j in range(pairs):
        q = drows[:, j * PAIR:(j + 1) * PAIR].astype(jnp.float32) * (HEAD ** (-0.5))
        swapped = pltpu.roll(q, HEAD, 1)
        both = jnp.concatenate(
            [jnp.where(lane_d < HEAD, q, 0.0), jnp.where(lane_d < HEAD, swapped, 0.0)], axis=0
        )
        dq[2 * j * dec_rows:(2 * j + 2) * dec_rows, :] = both.astype(jnp.bfloat16)
    q_step(1)
    enc_plane[1]()
    k_plane[1]()
    v_plane[1]()

    for t in range(2, n_q - 1):
        q_step(t)
    enc_plane[2]()
    d_total = heads * dec_rows
    d_chunk = min(256, d_total)

    def dec_step(i):
        rows = pl.ds(pl.multiple_of(i * d_chunk, d_chunk), d_chunk)
        kv = encbuf[...].reshape(n_seq * tokens, PAIR)
        s = dot_t(dq[rows, :], kv)
        p = jnp.exp(s - jnp.max(s, axis=1, keepdims=True))
        total = jnp.sum(p, axis=1, keepdims=True)
        do[rows, :] = dot(p.astype(jnp.bfloat16), kv) / total

    loop(0, d_total // d_chunk, dec_step)
    for j in range(pairs):
        even = do[2 * j * dec_rows:(2 * j + 1) * dec_rows, :]
        odd = do[(2 * j + 1) * dec_rows:(2 * j + 2) * dec_rows, :]
        dec[me_kv, me_q, :, j * PAIR:(j + 1) * PAIR] = jnp.where(
            lane_d < HEAD, pltpu.roll(even, HEAD, 1), odd
        ).astype(jnp.bfloat16)
    for d in range(1, n_q):
        dec_copy(d).start()

    low_half = lax.broadcasted_iota(jnp.int32, (tokens, PAIR), 1) < HEAD
    lane = lax.broadcasted_iota(jnp.int32, (tokens, PAIR), 1)
    if n_q > 2:
        q_step(n_q - 1)
    for d in range(1, n_q):
        dec_arrival(d).wait_recv()
    dec_plane[0]()
    k_plane[2]()
    v_plane[2]()
    for d in list(range(1, n_q)) + [0]:
        block = up(me_q, d, n_q)
        if d == 0:
            dec_plane[1]()

        def pair_step(j, stat):
            cols = pl.ds(pl.multiple_of(j * PAIR, PAIR), PAIR)
            q = stacked_pair(qbuf[block, :, cols], low_half)
            s = dot_t(q, kbuf[:, :, cols].reshape(n_kv * tokens, PAIR))
            if has_bias:
                s = s + bias_ref[0:1, :]
            peak = jnp.max(s, axis=1, keepdims=True)
            p = jnp.exp(s - peak)
            total = jnp.sum(p, axis=1, keepdims=True)
            o = dot(p.astype(jnp.bfloat16), vbuf[:, :, cols].reshape(n_kv * tokens, PAIR)) / total
            lse = peak + jnp.log(total)
            osend[block, :, cols] = jnp.where(low_half, o[:tokens], o[tokens:]).astype(jnp.bfloat16)
            stat = jnp.where(lane == 2 * j, lse[:tokens], stat)
            return jnp.where(lane == 2 * j + 1, lse[tokens:], stat)

        stat = lax.fori_loop(0, pairs, pair_step, jnp.zeros((tokens, PAIR), jnp.float32))
        ssend[block] = stat.T[:heads]
        if d:
            for copy in o_copy(d):
                copy.start()
        else:
            wts[0] = stat

    @pl.when(has_prev)
    def _():
        for copy in halo_copy(0):
            copy.wait_recv()

    @pl.when(jnp.logical_not(has_prev))
    def _():
        khalo[0] = jnp.zeros_like(kl)
        vhalo[0] = jnp.zeros_like(vl)

    @pl.when(has_next)
    def _():
        for copy in halo_copy(1):
            copy.wait_recv()

    @pl.when(jnp.logical_not(has_next))
    def _():
        khalo[1] = jnp.zeros_like(kl)
        vhalo[1] = jnp.zeros_like(vl)

    def light_step(j):
        cols = pl.ds(pl.multiple_of(j * PAIR, PAIR), PAIR)
        q = stacked_pair(ql[:, cols], low_half)
        keys = jnp.concatenate([khalo[0, :, cols], kl[:, cols], khalo[1, :, cols]], axis=0)
        rows = jnp.concatenate([vhalo[0, :, cols], vl[:, cols], vhalo[1, :, cols]], axis=0)
        mask = band[...]
        s = dot_t(q, keys) + jnp.concatenate([mask, mask], axis=0)
        p = jnp.exp(s - jnp.max(s, axis=1, keepdims=True))
        total = jnp.sum(p, axis=1, keepdims=True)
        o = dot(p.astype(jnp.bfloat16), rows) / total
        light[:, cols] = jnp.where(low_half, o[:tokens], o[tokens:])

    loop(0, pairs, light_step)

    for d in range(1, n_q):
        for copy in o_arrival(d):
            copy.wait_recv()
        pad = jnp.zeros((PAIR - heads, tokens), jnp.float32)
        wts[d] = jnp.concatenate([srecv[down(me_q, d, n_q)], pad], axis=0).T
    top = wts[0]
    for d in range(1, n_q):
        top = jnp.maximum(top, wts[d])
    norm = jnp.zeros_like(top)
    for d in range(n_q):
        share = jnp.exp(wts[d] - top)
        wts[d] = share
        norm = norm + share
    for d in range(n_q):
        wts[d] = wts[d] / norm

    def join_step(j):
        cols = pl.ds(pl.multiple_of(j * PAIR, PAIR), PAIR)
        acc = jnp.zeros((tokens, PAIR), jnp.float32)
        for d in range(n_q):
            part = osend[me_q, :, cols] if d == 0 else orecv[down(me_q, d, n_q), :, cols]
            w = wts[d]
            even = jnp.sum(jnp.where(lane == 2 * j, w, 0.0), axis=1, keepdims=True)
            odd = jnp.sum(jnp.where(lane == 2 * j + 1, w, 0.0), axis=1, keepdims=True)
            acc = acc + jnp.where(low_half, even, odd) * part.astype(jnp.float32)
        heavy = acc.astype(jnp.bfloat16).astype(jnp.float32)
        out[:, cols] = (light[:, cols] + heavy).astype(jnp.bfloat16)

    loop(0, pairs, join_step)

    dec_plane[2]()
    for part in (enc_plane, dec_plane, k_plane, v_plane):
        part[3]()
    for d in range(1, n_q):
        enc_copy(d).wait_send()
        dec_copy(d).wait_send()
        for copy in o_copy(d):
            copy.wait_send()

    @pl.when(has_up)
    def _():
        own_q(1).wait_send()

    @pl.when(has_down)
    def _():
        own_q(-1).wait_send()

    for t in range(1, n_q - 1):
        for way in (1, -1):
            src = me_q - way * t

            @pl.when((src >= 0) & (src < n_q) & (me_q + way >= 0) & (me_q + way < n_q))
            def _():
                q_copy(jnp.clip(src, 0, n_q - 1), way).wait_send()

    @pl.when(has_next)
    def _():
        for copy in halo_copy(0):
            copy.wait_send()

    @pl.when(has_prev)
    def _():
        for copy in halo_copy(1):
            copy.wait_send()


def local(
    q_light, k_light, v_light, q_heavy, k_heavy, v_heavy, enc_kv, dec_queries, query_ids, key_ids
):
    _, tokens, width = q_light.shape
    n_coarse = lax.axis_size("coarse")
    n_fine = lax.axis_size("fine")
    n_seq = n_coarse * n_fine
    n_q = n_fine // LOW
    n_kv = n_coarse * LOW
    heads = width // HEAD
    count = dec_queries.shape[1]
    dec_rows = count // n_seq
    mine = dec_queries.reshape(n_kv, n_q, dec_rows, width)
    args = [q_light[0], k_light[0], v_light[0], q_heavy[0], k_heavy[0], v_heavy[0], enc_kv[0], mine]
    has_bias = key_ids.shape[1] != n_seq
    if has_bias:
        high = lax.div(lax.axis_index("fine"), LOW)
        member = jnp.arange(n_kv, dtype=jnp.int32)
        blocks = (member // LOW) * n_fine + high * LOW + member % LOW
        listed = jnp.any(blocks[:, None] == key_ids[0][None, :], axis=1)
        bias = jnp.repeat(jnp.where(listed, 0.0, NEG).astype(jnp.float32), tokens)
        args.append(jnp.broadcast_to(bias[None], (8, n_kv * tokens)))
    bf16, f32 = jnp.bfloat16, jnp.float32
    dma = pltpu.SemaphoreType.DMA
    vmem = pl.BlockSpec(memory_space=pltpu.VMEM)
    encoded, decoded = pl.pallas_call(
        functools.partial(kernel, (n_coarse, n_fine, tokens, width, dec_rows), has_bias),
        out_shape=(
            jax.ShapeDtypeStruct((tokens, width), bf16),
            jax.ShapeDtypeStruct((n_kv, n_q, dec_rows, width), bf16),
        ),
        in_specs=[vmem] * 7 + [pl.BlockSpec(memory_space=pl.ANY)] + [vmem] * (len(args) - 8),
        out_specs=(vmem, vmem),
        scratch_shapes=[
            pltpu.VMEM((n_kv, n_q, tokens, PAIR), bf16),
            pltpu.VMEM((heads * dec_rows, PAIR), bf16),
            pltpu.VMEM((heads * dec_rows, PAIR), f32),
            pltpu.VMEM((n_q, tokens, width), bf16),
            pltpu.VMEM((n_kv, tokens, width), bf16),
            pltpu.VMEM((n_kv, tokens, width), bf16),
            pltpu.VMEM((2, tokens, width), bf16),
            pltpu.VMEM((2, tokens, width), bf16),
            pltpu.VMEM((n_q, tokens, width), bf16),
            pltpu.VMEM((n_q, tokens, width), bf16),
            pltpu.VMEM((n_q, heads, tokens), f32),
            pltpu.VMEM((n_q, heads, tokens), f32),
            pltpu.VMEM((n_q, tokens, PAIR), f32),
            pltpu.VMEM((tokens, width), f32),
            pltpu.VMEM((tokens, 3 * tokens), f32),
            dma((n_q,)), dma((n_q,)),
            dma((n_q,)), dma((n_q,)),
            dma((n_q + 2,)), dma((n_q,)),
            dma((n_q,)), dma((n_q,)),
            dma((n_q,)), dma((n_q,)),
            dma((2, 2)), dma((2, 2)),
            dma((2, n_coarse)), dma((n_kv,)),
            dma((2, n_coarse)), dma((n_kv,)),
            dma((2, n_coarse)), dma((n_kv,)),
            dma((2, n_coarse)), dma((n_kv,)),
            pltpu.VMEM((dec_rows, width), bf16), dma,
        ],
        compiler_params=pltpu.CompilerParams(
            collective_id=0, has_side_effects=True, vmem_limit_bytes=60 * 1024 * 1024
        ),
    )(*args)
    return encoded[None], decoded.reshape(1, count, width)


def solution(mesh):
    rows = P("doc", ("coarse", "fine"), None)
    placed = (rows,) * 7 + (P("doc", None, None), P("doc", None), P("doc", None))
    return jax.shard_map(
        local,
        mesh=mesh,
        in_specs=placed,
        out_specs=(rows, P("doc", None, None)),
        check_vma=False,
    )
```
